32 devices in a mesh: tok: 8 (over z, x), wid: 4 (over y, core).
Axes of the slice: x: 2, y: 2, z: 4, core: 2. Of those that a mesh axis runs over, the one named last changes fastest.
Arguments:
- acts: bfloat16 [3072, 53248], P('tok', 'wid'), may hold values from -100 to 100
- out_grads: bfloat16 [3072, 16384], P('tok', 'wid'), may hold values from -6 to 6
- test_matrix: bfloat16 [16384, 256], P('wid'), may hold values from -1 to 1
Outputs:
- coeffs: float32 [256, 16384], P('tok', 'wid')
The draws below stay inside these ranges and needn't reach their ends.
All inputs are finite; a program needn't handle non-finite values.
Results may differ from the reference program's by a relative error of at most 0.01.
Values may be sent and summed in bfloat16 or wider, within the bound.
A program may use at most 64 MiB of HBM per device.

```python
import math
import jax
import jax.numpy as jnp
from jax import lax

D = 16384
F = 53248
R = 256
TOK_DEV = 384
TOKENS = 3072
N_TOK = 8


def base_values(key, shape):
    return jnp.clip(jax.random.normal(key, shape, jnp.float32), -6.0, 6.0)


def draw_acts(key, part):
    first = jax.random.fold_in(key, 11)
    second = jax.random.fold_in(key, 12)
    values = base_values(first, (TOKENS, F))
    position = jnp.arange(F, dtype=jnp.float32) / (F - 1)
    rough = jax.random.uniform(second, (F,), jnp.float32, 0.6, 1.4)
    column = jnp.exp(position * math.log(10.0)) * rough
    scaled = values * column[None, :]
    return scaled.astype(jnp.bfloat16)


def draw_out_grads(key, part):
    first = jax.random.fold_in(key, 21)
    values = base_values(first, (TOKENS, D))
    return values.astype(jnp.bfloat16)


def draw_test_matrix(key, part):
    first = jax.random.fold_in(key, 31)
    values = base_values(first, (D, R))
    return (values * (1.0 / math.sqrt(D))).astype(jnp.bfloat16)


def setup_inputs(seed: int = 0) -> dict:
    seeds = jax.random.split(jax.random.key(seed), 4)
    acts = draw_acts(jax.random.fold_in(seeds[3], 71), 0)
    out_grads = draw_out_grads(jax.random.fold_in(seeds[3], 71), 0)
    test_matrix = draw_test_matrix(jax.random.fold_in(seeds[3], 71), 0)
    return dict(acts=acts, out_grads=out_grads, test_matrix=test_matrix)


def reference(acts, out_grads, test_matrix):
    probe = jnp.dot(out_grads.astype(jnp.float32), test_matrix.astype(jnp.float32), preferred_element_type=jnp.float32).astype(jnp.bfloat16)
    acts_blocks = acts.reshape(N_TOK, TOK_DEV, F)
    probe_blocks = probe.reshape(N_TOK, TOK_DEV, R)

    def add_block(total, pair):
        block_acts, block_probe = pair
        term = lax.dot_general(block_acts.astype(jnp.float32), block_probe.astype(jnp.float32), (((0,), (0,)), ((), ())), preferred_element_type=jnp.float32)
        term = lax.optimization_barrier(term.astype(jnp.bfloat16))
        return (total + term.astype(jnp.float32), None)
    sketch, unused = lax.scan(add_block, jnp.zeros((F, R), jnp.float32), (acts_blocks, probe_blocks))
    gram = jnp.dot(sketch.T, sketch, precision=lax.Precision.HIGHEST)
    lower = jnp.linalg.cholesky(gram)
    inverse = lax.linalg.triangular_solve(lower, jnp.eye(R, dtype=jnp.float32), left_side=True, lower=True)
    basis = jnp.dot(sketch, inverse.T, precision=lax.Precision.HIGHEST).astype(jnp.bfloat16)
    proj = jnp.dot(acts.astype(jnp.float32), basis.astype(jnp.float32), preferred_element_type=jnp.float32).astype(jnp.bfloat16)
    coeffs = lax.dot_general(proj.astype(jnp.float32), out_grads.astype(jnp.float32), (((0,), (0,)), ((), ())), preferred_element_type=jnp.float32)
    return coeffs * (1.0 / math.sqrt(TOKENS))
```

```python
import functools
import math

import jax
import jax.numpy as jnp
from jax import lax
from jax.experimental import pallas as pl
from jax.experimental.pallas import tpu as pltpu
from jax.sharding import PartitionSpec as P

MESH = pl.DeviceIdType.MESH
F32 = jnp.float32
BF16 = jnp.bfloat16
VMEM_LIMIT = 60 * 1024 * 1024
WAYS = (0, 1)
PIECES = 2


def nt(a, b, precision=None):
    return lax.dot_general(
        a, b, (((1,), (1,)), ((), ())), preferred_element_type=F32, precision=precision
    )


class Ring:
    def __init__(self, n):
        self.n, self.rows, self.cols = n, 4, n // 4
        self.body = self.rows * (self.cols - 1)
        self.tok = lax.axis_index("tok")
        self.pos = self.pos_of(self.tok)

    def pos_of(self, tok):
        r, c = lax.div(tok, self.cols), lax.rem(tok, self.cols)
        odd = lax.rem(r, 2)
        inner = lax.div(c + self.cols - 1, self.cols)
        along = r * (self.cols - 1) + (1 - odd) * (c - 1) + odd * (self.cols - 1 - c)
        back = self.body + self.rows - 1 - r
        return inner * along + (1 - inner) * back

    def tok_of(self, pos):
        last = lax.div(pos, self.body)
        r, k = lax.div(pos, self.cols - 1), lax.rem(pos, self.cols - 1)
        odd = lax.rem(r, 2)
        along = r * self.cols + (1 - odd) * (k + 1) + odd * (self.cols - 1 - k)
        back = (self.rows - 1 - (pos - self.body)) * self.cols
        return (1 - last) * along + last * back

    def at(self, offset):
        return lax.rem(self.pos + offset + 2 * self.n, self.n)

    def neighbours(self):
        return self.tok_of(self.at(1)), self.tok_of(self.at(-1))

    def barrier(self):
        sem = pltpu.get_barrier_semaphore()
        for other in self.neighbours():
            pl.semaphore_signal(
                sem, inc=1, device_id={"tok": other}, device_id_type=MESH
            )
        pl.semaphore_wait(sem, 2)


def ring_scatter(ring, term, store, send, recv, send_sems, recv_sems):
    n = ring.n
    dest = ring.neighbours()

    def copy(way, step, piece):
        return pltpu.make_async_remote_copy(
            src_ref=send.at[way, step, piece],
            dst_ref=recv.at[way, step, piece],
            send_sem=send_sems.at[way, step, piece],
            recv_sem=recv_sems.at[way, step, piece],
            device_id={"tok": dest[way]},
            device_id_type=MESH,
        )

    def block(way, step):
        return ring.at(-1 - step) if way == 0 else ring.at(1 + step)

    for piece in range(PIECES):
        for way in WAYS:
            send[way, 0, piece] = term(way, piece, block(way, 0)).astype(BF16)
            copy(way, 0, piece).start()

    def step(s, carry):
        for piece in range(PIECES):
            for way in WAYS:
                own = term(way, piece, block(way, s))
                copy(way, s - 1, piece).wait_recv()
                total = own + recv[way, s - 1, piece].astype(F32)
                send[way, s, piece] = total.astype(BF16)
                copy(way, s, piece).start()
        return carry

    lax.fori_loop(1, n - 1, step, 0)
    for piece in range(PIECES):
        for way in WAYS:
            own = term(way, piece, ring.pos)
            copy(way, n - 2, piece).wait_recv()
            store(way, piece, own + recv[way, n - 2, piece].astype(F32))

    def drain(s, carry):
        for piece in range(PIECES):
            for way in WAYS:
                copy(way, s, piece).wait_send()
        return carry

    lax.fori_loop(0, n - 1, drain, 0)


def sketch_kernel(n, acts, probe_t, out, send, recv, send_sems, recv_sems):
    ring = Ring(n)
    width = out.shape[1]
    rows = out.shape[0] // (2 * PIECES)

    def term(way, piece, pos):
        first = (way * PIECES + piece) * rows
        columns = pl.ds(pl.multiple_of(pos * width, 128), width)
        return jnp.dot(
            probe_t[first : first + rows, :], acts[:, columns], preferred_element_type=F32
        )

    def store(way, piece, total):
        first = (way * PIECES + piece) * rows
        out[first : first + rows, :] = total.astype(BF16)

    ring.barrier()
    ring_scatter(ring, term, store, send, recv, send_sems, recv_sems)


def gather_kernel(n, acts, own, mixed, gram, held, send_sems, recv_sems):
    ring = Ring(n)
    width = own.shape[1]
    rows = own.shape[0] // (2 * PIECES)
    half = own.shape[0] // 2
    dest = ring.neighbours()

    def copy(way, step, piece, first=False):
        pos = ring.at(-step) if way == 0 else ring.at(step)
        lines = pl.ds((way * PIECES + piece) * rows, rows)
        return pltpu.make_async_remote_copy(
            src_ref=own.at[lines] if first else held.at[pos, lines],
            dst_ref=held.at[pos, lines],
            send_sem=send_sems.at[way, step, piece],
            recv_sem=recv_sems.at[way, step, piece],
            device_id={"tok": dest[way]},
            device_id_type=MESH,
        )

    def add(way, pos, ref):
        columns = pl.ds(pl.multiple_of(pos * width, 128), width)
        lanes = slice(way * half, (way + 1) * half)
        mixed[:, lanes] += nt(acts[:, columns], ref[lanes, :])

    ring.barrier()
    for piece in range(PIECES):
        for way in WAYS:
            copy(way, 0, piece, True).start()
    mixed[...] = jnp.zeros_like(mixed)
    gram[...] = nt(own[...], own[...])
    for way in WAYS:
        add(way, ring.pos, own)

    def step(s, carry):
        for piece in range(PIECES):
            for way in WAYS:
                copy(way, s - 1, piece).wait_recv()
                copy(way, s, piece).start()
        for way in WAYS:
            pos = ring.at(-s) if way == 0 else ring.at(s)
            add(way, pos, held.at[pos])
        return carry

    lax.fori_loop(1, n - 1, step, 0)
    for piece in range(PIECES):
        for way in WAYS:
            copy(way, n - 2, piece).wait_recv()
    for way in WAYS:
        pos = ring.at(1 - n) if way == 0 else ring.at(n - 1)
        add(way, pos, held.at[pos])

    def more(s, carry):
        block = held.at[ring.at(s)]
        gram[...] += nt(block[...], block[...])
        return carry

    lax.fori_loop(1, n, more, 0)

    def drain(s, carry):
        for piece in range(PIECES):
            for way in WAYS:
                copy(way, s, piece, False).wait_send()
        return carry

    lax.fori_loop(0, n - 1, drain, 0)


def coeffs_kernel(n, scale, mixed, inverse, grads, out, terms, send, recv, send_sems, recv_sems):
    ring = Ring(n)
    rows, width = out.shape
    part = width // (2 * PIECES)

    def term(way, piece, pos):
        first = (way * PIECES + piece) * part
        return terms[ring.tok_of(pos), :, first : first + part]

    def store(way, piece, total):
        first = (way * PIECES + piece) * part
        out[:, first : first + part] = total

    ring.barrier()
    proj_t = nt(inverse[...], mixed[...], lax.Precision.HIGHEST).astype(BF16)
    for first in range(0, width, 512 if width % 512 == 0 else width):
        last = min(width, first + 512) if width % 512 == 0 else width
        piece = jnp.dot(proj_t, grads[:, first:last], preferred_element_type=F32)
        terms[:, :, first:last] = (piece * scale).reshape(n, rows, last - first)
    ring_scatter(ring, term, store, send, recv, send_sems, recv_sems)


def call(kernel, outs, scratch, number, *args):
    vmem = pl.BlockSpec(memory_space=pltpu.VMEM)
    return pl.pallas_call(
        kernel,
        out_shape=outs,
        in_specs=[vmem] * len(args),
        out_specs=jax.tree.map(lambda _: vmem, outs),
        scratch_shapes=scratch,
        compiler_params=pltpu.CompilerParams(
            collective_id=number, has_side_effects=True, vmem_limit_bytes=VMEM_LIMIT
        ),
    )(*args)


def sems(n):
    return [pltpu.SemaphoreType.DMA((2, n - 1, PIECES)) for _ in range(2)]


def slots(n, rows, width):
    return [pltpu.VMEM((2, n - 1, PIECES, rows, width), BF16) for _ in range(2)]


def factor_inverse(gram):
    lower = jnp.linalg.cholesky(gram)
    eye_matrix = jnp.eye(gram.shape[0], dtype=F32)
    return lax.linalg.triangular_solve(lower, eye_matrix, left_side=True, lower=True)


def ring_shards(n, acts, out_grads, test_matrix):
    partial_probe = jnp.dot(out_grads, test_matrix, preferred_element_type=F32)
    probe = lax.psum(partial_probe, "wid").astype(BF16)
    tokens, hidden = acts.shape
    rank, model = test_matrix.shape[1], out_grads.shape[1]
    width = hidden // n
    struct = jax.ShapeDtypeStruct
    rows_t = call(
        functools.partial(sketch_kernel, n),
        struct((rank, width), BF16),
        slots(n, rank // (2 * PIECES), width) + sems(n),
        0, acts, probe.T,
    )
    mixed_part, gram_part = call(
        functools.partial(gather_kernel, n),
        [struct((tokens, rank), F32), struct((rank, rank), F32)],
        [pltpu.VMEM((n, rank, width), BF16)] + sems(n),
        1, acts, rows_t,
    )
    both = lax.psum(jnp.concatenate([mixed_part, gram_part]), "wid")
    mixed, gram = both[:tokens], both[tokens:]
    inverse = factor_inverse(gram)
    scale = 1.0 / math.sqrt(tokens * n)
    rows = rank // n
    return call(
        functools.partial(coeffs_kernel, n, scale),
        struct((rows, model), F32),
        [pltpu.VMEM((n, rows, model), F32)]
        + slots(n, rows, model // (2 * PIECES)) + sems(n),
        2, mixed, inverse, out_grads,
    )


def plain_shards(acts, out_grads, test_matrix):
    partial_probe = jnp.dot(out_grads, test_matrix, preferred_element_type=F32)
    probe = lax.psum(partial_probe, "wid").astype(BF16)
    local_sketch = lax.dot_general(
        acts, probe, (((0,), (0,)), ((), ())), preferred_element_type=F32
    )
    sketch = lax.psum(local_sketch.astype(BF16), "tok")
    gram = lax.psum(
        lax.dot_general(sketch, sketch, (((0,), (0,)), ((), ())), preferred_element_type=F32),
        "wid",
    )
    inverse = factor_inverse(gram)
    mixed = lax.psum(jnp.dot(acts, sketch, preferred_element_type=F32), "wid")
    proj = jnp.dot(mixed, inverse.T, precision=lax.Precision.HIGHEST).astype(BF16)
    scale = 1.0 / math.sqrt(acts.shape[0] * lax.axis_size("tok"))
    term = lax.dot_general(
        proj, out_grads, (((0,), (0,)), ((), ())), preferred_element_type=F32
    )
    return lax.psum_scatter(term * scale, "tok", scatter_dimension=0, tiled=True)


def solution(mesh):
    n = mesh.shape["tok"]

    def shards(acts, out_grads, test_matrix):
        width, left = divmod(acts.shape[1], n)
        if n % 4 == 0 and n > 4 and left == 0 and width % 128 == 0:
            return ring_shards(n, acts, out_grads, test_matrix)
        return plain_shards(acts, out_grads, test_matrix)

    return jax.shard_map(
        shards,
        mesh=mesh,
        in_specs=(P("tok", "wid"), P("tok", "wid"), P("wid", None)),
        out_specs=P("tok", "wid"),
        check_vma=False,
    )
```

```python
import functools
import math

import jax
import jax.numpy as jnp
from jax import lax
from jax.experimental import pallas as pl
from jax.experimental.pallas import tpu as pltpu
from jax.sharding import PartitionSpec as P

MESH = pl.DeviceIdType.MESH
F32 = jnp.float32
BF16 = jnp.bfloat16
VMEM_LIMIT = 60 * 1024 * 1024
WAYS = (0, 1)
PIECES = 2


def nt(a, b, precision=None):
    return lax.dot_general(
        a, b, (((1,), (1,)), ((), ())), preferred_element_type=F32, precision=precision
    )


class Ring:
    def __init__(self, n):
        self.n, self.rows, self.cols = n, 4, n // 4
        self.body = self.rows * (self.cols - 1)
        self.tok = lax.axis_index("tok")
        self.pos = self.pos_of(self.tok)

    def pos_of(self, tok):
        r, c = lax.div(tok, self.cols), lax.rem(tok, self.cols)
        odd = lax.rem(r, 2)
        inner = lax.div(c + self.cols - 1, self.cols)
        along = r * (self.cols - 1) + (1 - odd) * (c - 1) + odd * (self.cols - 1 - c)
        back = self.body + self.rows - 1 - r
        return inner * along + (1 - inner) * back

    def tok_of(self, pos):
        last = lax.div(pos, self.body)
        r, k = lax.div(pos, self.cols - 1), lax.rem(pos, self.cols - 1)
        odd = lax.rem(r, 2)
        along = r * self.cols + (1 - odd) * (k + 1) + odd * (self.cols - 1 - k)
        back = (self.rows - 1 - (pos - self.body)) * self.cols
        return (1 - last) * along + last * back

    def at(self, offset):
        return lax.rem(self.pos + offset + 2 * self.n, self.n)

    def neighbours(self):
        return self.tok_of(self.at(1)), self.tok_of(self.at(-1))

    def barrier(self, peers=1):
        sem = pltpu.get_barrier_semaphore()
        me = lax.axis_index("wid")
        for k in range(1, peers):
            other = lax.rem(me + k, peers)
            pl.semaphore_signal(
                sem, inc=1, device_id={"wid": other}, device_id_type=MESH
            )
        for other in self.neighbours():
            pl.semaphore_signal(
                sem, inc=1, device_id={"tok": other}, device_id_type=MESH
            )
        pl.semaphore_wait(sem, 1 + peers)


def wid_sum(m, part, got, mine, out, sems):
    me = lax.axis_index("wid")
    share = part.shape[0] // m

    def lines(index):
        return pl.ds(pl.multiple_of(index * share, 16), share)

    def copy(phase, k):
        other = lax.rem(me + k, m)
        return pltpu.make_async_remote_copy(
            src_ref=mine if phase else part.at[lines(other)],
            dst_ref=out.at[lines(me)] if phase else got.at[k - 1],
            send_sem=sems.at[phase, 0, k - 1],
            recv_sem=sems.at[phase, 1, k - 1],
            device_id={"wid": other},
            device_id_type=MESH,
        )

    for k in range(1, m):
        copy(0, k).start()
    total = part[lines(me), :]
    for k in range(1, m):
        copy(0, k).wait_recv()
        total = total + got[k - 1]
    mine[...] = total.astype(mine.dtype)
    for k in range(1, m):
        copy(1, k).start()
    out[lines(me), :] = total.astype(out.dtype)
    for k in range(1, m):
        copy(0, k).wait_send()
        copy(1, k).wait()


def ring_scatter(ring, term, store, send, recv, send_sems, recv_sems):
    n = ring.n
    dest = ring.neighbours()

    def copy(way, step, piece):
        return pltpu.make_async_remote_copy(
            src_ref=send.at[way, step, piece],
            dst_ref=recv.at[way, step, piece],
            send_sem=send_sems.at[way, step, piece],
            recv_sem=recv_sems.at[way, step, piece],
            device_id={"tok": dest[way]},
            device_id_type=MESH,
        )

    def block(way, step):
        return ring.at(-1 - step) if way == 0 else ring.at(1 + step)

    for piece in range(PIECES):
        for way in WAYS:
            send[way, 0, piece] = term(way, piece, block(way, 0)).astype(BF16)
            copy(way, 0, piece).start()

    def step(s, carry):
        for piece in range(PIECES):
            for way in WAYS:
                own = term(way, piece, block(way, s))
                copy(way, s - 1, piece).wait_recv()
                total = own + recv[way, s - 1, piece].astype(F32)
                send[way, s, piece] = total.astype(BF16)
                copy(way, s, piece).start()
        return carry

    lax.fori_loop(1, n - 1, step, 0)
    for piece in range(PIECES):
        for way in WAYS:
            own = term(way, piece, ring.pos)
            copy(way, n - 2, piece).wait_recv()
            store(way, piece, own + recv[way, n - 2, piece].astype(F32))

    def drain(s, carry):
        for piece in range(PIECES):
            for way in WAYS:
                copy(way, s, piece).wait_send()
        return carry

    lax.fori_loop(0, n - 1, drain, 0)


def sketch_kernel(
    n, m, acts, grads, test, out, part, got, mine, probe_t, wid_sems,
    send, recv, send_sems, recv_sems,
):
    ring = Ring(n)
    width = out.shape[1]
    rows = out.shape[0] // (2 * PIECES)

    def term(way, piece, pos):
        first = (way * PIECES + piece) * rows
        columns = pl.ds(pl.multiple_of(pos * width, 128), width)
        return jnp.dot(
            probe_t[first : first + rows, :], acts[:, columns], preferred_element_type=F32
        )

    def store(way, piece, total):
        first = (way * PIECES + piece) * rows
        out[first : first + rows, :] = total.astype(BF16)

    ring.barrier(m)
    part[...] = jnp.dot(grads[...], test[...], preferred_element_type=F32).T
    wid_sum(m, part, got, mine, probe_t, wid_sems)
    ring_scatter(ring, term, store, send, recv, send_sems, recv_sems)


def gather_kernel(
    n, m, acts, own, out_mixed, out_gram, part, got, mine, full, wid_sems,
    held, send_sems, recv_sems,
):
    tokens = acts.shape[0]
    mixed, gram = part.at[0:tokens], part.at[tokens : part.shape[0]]
    ring = Ring(n)
    width = own.shape[1]
    rows = own.shape[0] // (2 * PIECES)
    half = own.shape[0] // 2
    dest = ring.neighbours()

    def copy(way, step, piece, first=False):
        pos = ring.at(-step) if way == 0 else ring.at(step)
        lines = pl.ds((way * PIECES + piece) * rows, rows)
        return pltpu.make_async_remote_copy(
            src_ref=own.at[lines] if first else held.at[pos, lines],
            dst_ref=held.at[pos, lines],
            send_sem=send_sems.at[way, step, piece],
            recv_sem=recv_sems.at[way, step, piece],
            device_id={"tok": dest[way]},
            device_id_type=MESH,
        )

    def add(way, pos, ref):
        columns = pl.ds(pl.multiple_of(pos * width, 128), width)
        lanes = slice(way * half, (way + 1) * half)
        mixed[:, lanes] += nt(acts[:, columns], ref[lanes, :])

    ring.barrier(m)
    for piece in range(PIECES):
        for way in WAYS:
            copy(way, 0, piece, True).start()
    mixed[...] = jnp.zeros_like(mixed)
    gram[...] = nt(own[...], own[...])
    for way in WAYS:
        add(way, ring.pos, own)

    def step(s, carry):
        for piece in range(PIECES):
            for way in WAYS:
                copy(way, s - 1, piece).wait_recv()
                copy(way, s, piece).start()
        for way in WAYS:
            pos = ring.at(-s) if way == 0 else ring.at(s)
            add(way, pos, held.at[pos])
        return carry

    lax.fori_loop(1, n - 1, step, 0)
    for piece in range(PIECES):
        for way in WAYS:
            copy(way, n - 2, piece).wait_recv()
    for way in WAYS:
        pos = ring.at(1 - n) if way == 0 else ring.at(n - 1)
        add(way, pos, held.at[pos])

    def more(s, carry):
        block = held.at[ring.at(s)]
        gram[...] += nt(block[...], block[...])
        return carry

    lax.fori_loop(1, n, more, 0)
    wid_sum(m, part, got, mine, full, wid_sems)
    out_mixed[...] = full[0:tokens, :]
    out_gram[...] = full[tokens : part.shape[0], :]

    def drain(s, carry):
        for piece in range(PIECES):
            for way in WAYS:
                copy(way, s, piece, False).wait_send()
        return carry

    lax.fori_loop(0, n - 1, drain, 0)


def invert(lower, inverse):
    i = lax.broadcasted_iota(jnp.int32, lower.shape, 0)
    j = lax.broadcasted_iota(jnp.int32, lower.shape, 1)
    inverse[...] = jnp.where(i == j, 1.0 / jnp.where(i == j, lower[...], 1.0), 0.0)

    def level(k, carry):
        i_block, j_block = lax.shift_right_logical(i, k), lax.shift_right_logical(j, k)
        same = lax.shift_right_logical(i, k + 1) == lax.shift_right_logical(j, k + 1)
        below = jnp.where(jnp.logical_and(same, i_block > j_block), lower[...], 0.0)
        high = lax.Precision.HIGHEST
        right = jnp.dot(below, inverse[...], precision=high, preferred_element_type=F32)
        inverse[...] -= jnp.dot(
            inverse[...], right, precision=high, preferred_element_type=F32
        )
        return carry

    lax.fori_loop(0, (lower.shape[0] - 1).bit_length(), level, 0)


def coeffs_kernel(
    n, scale, mixed, lower, grads, out, inverse, terms, send, recv, send_sems, recv_sems
):
    ring = Ring(n)
    rows, width = out.shape
    part = width // (2 * PIECES)

    def term(way, piece, pos):
        first = (way * PIECES + piece) * part
        return terms[ring.tok_of(pos), :, first : first + part]

    def store(way, piece, total):
        first = (way * PIECES + piece) * part
        out[:, first : first + part] = total

    ring.barrier()
    invert(lower, inverse)
    proj_t = nt(inverse[...], mixed[...], lax.Precision.HIGHEST).astype(BF16)
    for first in range(0, width, 512 if width % 512 == 0 else width):
        last = min(width, first + 512) if width % 512 == 0 else width
        piece = jnp.dot(proj_t, grads[:, first:last], preferred_element_type=F32)
        terms[:, :, first:last] = (piece * scale).reshape(n, rows, last - first)
    ring_scatter(ring, term, store, send, recv, send_sems, recv_sems)


def call(kernel, outs, scratch, number, *args):
    vmem = pl.BlockSpec(memory_space=pltpu.VMEM)
    return pl.pallas_call(
        kernel,
        out_shape=outs,
        in_specs=[vmem] * len(args),
        out_specs=jax.tree.map(lambda _: vmem, outs),
        scratch_shapes=scratch,
        compiler_params=pltpu.CompilerParams(
            collective_id=number, has_side_effects=True, vmem_limit_bytes=VMEM_LIMIT
        ),
    )(*args)


def sems(n):
    return [pltpu.SemaphoreType.DMA((2, n - 1, PIECES)) for _ in range(2)]


def slots(n, rows, width):
    return [pltpu.VMEM((2, n - 1, PIECES, rows, width), BF16) for _ in range(2)]


def factor_inverse(gram):
    lower = jnp.linalg.cholesky(gram)
    eye_matrix = jnp.eye(gram.shape[0], dtype=F32)
    return lax.linalg.triangular_solve(lower, eye_matrix, left_side=True, lower=True)


def wid_scratch(m, rows, width, dtype):
    return [
        pltpu.VMEM((rows, width), F32),
        pltpu.VMEM((m - 1, rows // m, width), F32),
        pltpu.VMEM((rows // m, width), dtype),
        pltpu.VMEM((rows, width), dtype),
        pltpu.SemaphoreType.DMA((2, 2, m - 1)),
    ]


def ring_shards(n, m, acts, out_grads, test_matrix):
    tokens, hidden = acts.shape
    rank, model = test_matrix.shape[1], out_grads.shape[1]
    width = hidden // n
    struct = jax.ShapeDtypeStruct
    rows_t = call(
        functools.partial(sketch_kernel, n, m),
        struct((rank, width), BF16),
        wid_scratch(m, rank, tokens, BF16)
        + slots(n, rank // (2 * PIECES), width) + sems(n),
        0, acts, out_grads, test_matrix,
    )
    mixed, gram = call(
        functools.partial(gather_kernel, n, m),
        [struct((tokens, rank), F32), struct((rank, rank), F32)],
        wid_scratch(m, tokens + rank, rank, F32)
        + [pltpu.VMEM((n, rank, width), BF16)] + sems(n),
        1, acts, rows_t,
    )
    lower = jnp.linalg.cholesky(gram)
    scale = 1.0 / math.sqrt(tokens * n)
    rows = rank // n
    return call(
        functools.partial(coeffs_kernel, n, scale),
        struct((rows, model), F32),
        [pltpu.VMEM((rank, rank), F32), pltpu.VMEM((n, rows, model), F32)]
        + slots(n, rows, model // (2 * PIECES)) + sems(n),
        2, mixed, lower, out_grads,
    )


def plain_shards(acts, out_grads, test_matrix):
    partial_probe = jnp.dot(out_grads, test_matrix, preferred_element_type=F32)
    probe = lax.psum(partial_probe, "wid").astype(BF16)
    local_sketch = lax.dot_general(
        acts, probe, (((0,), (0,)), ((), ())), preferred_element_type=F32
    )
    sketch = lax.psum(local_sketch.astype(BF16), "tok")
    gram = lax.psum(
        lax.dot_general(sketch, sketch, (((0,), (0,)), ((), ())), preferred_element_type=F32),
        "wid",
    )
    inverse = factor_inverse(gram)
    mixed = lax.psum(jnp.dot(acts, sketch, preferred_element_type=F32), "wid")
    proj = jnp.dot(mixed, inverse.T, precision=lax.Precision.HIGHEST).astype(BF16)
    scale = 1.0 / math.sqrt(acts.shape[0] * lax.axis_size("tok"))
    term = lax.dot_general(
        proj, out_grads, (((0,), (0,)), ((), ())), preferred_element_type=F32
    )
    return lax.psum_scatter(term * scale, "tok", scatter_dimension=0, tiled=True)


def solution(mesh):
    n, m = mesh.shape["tok"], mesh.shape["wid"]

    def shards(acts, out_grads, test_matrix):
        width, left = divmod(acts.shape[1], n)
        even = acts.shape[0] % (16 * m) == 0 and test_matrix.shape[1] % (16 * m) == 0
        if n % 4 == 0 and n > 4 and m > 1 and even and left == 0 and width % 128 == 0:
            return ring_shards(n, m, acts, out_grads, test_matrix)
        return plain_shards(acts, out_grads, test_matrix)

    return jax.shard_map(
        shards,
        mesh=mesh,
        in_specs=(P("tok", "wid"), P("tok", "wid"), P("wid", None)),
        out_specs=P("tok", "wid"),
        check_vma=False,
    )
```

```python
import functools
import math

import jax
import jax.numpy as jnp
from jax import lax
from jax.experimental import pallas as pl
from jax.experimental.pallas import tpu as pltpu
from jax.sharding import PartitionSpec as P

MESH = pl.DeviceIdType.MESH
F32 = jnp.float32
BF16 = jnp.bfloat16
VMEM_LIMIT = 60 * 1024 * 1024
WAYS = (0, 1)
PIECES = 2


def nt(a, b, precision=None):
    return lax.dot_general(
        a, b, (((1,), (1,)), ((), ())), preferred_element_type=F32, precision=precision
    )


class Ring:
    def __init__(self, n):
        self.n, self.rows, self.cols = n, 4, n // 4
        self.body = self.rows * (self.cols - 1)
        self.tok = lax.axis_index("tok")
        self.pos = self.pos_of(self.tok)

    def pos_of(self, tok):
        r, c = lax.div(tok, self.cols), lax.rem(tok, self.cols)
        odd = lax.rem(r, 2)
        inner = lax.div(c + self.cols - 1, self.cols)
        along = r * (self.cols - 1) + (1 - odd) * (c - 1) + odd * (self.cols - 1 - c)
        back = self.body + self.rows - 1 - r
        return inner * along + (1 - inner) * back

    def tok_of(self, pos):
        last = lax.div(pos, self.body)
        r, k = lax.div(pos, self.cols - 1), lax.rem(pos, self.cols - 1)
        odd = lax.rem(r, 2)
        along = r * self.cols + (1 - odd) * (k + 1) + odd * (self.cols - 1 - k)
        back = (self.rows - 1 - (pos - self.body)) * self.cols
        return (1 - last) * along + last * back

    def at(self, offset):
        return lax.rem(self.pos + offset + 2 * self.n, self.n)

    def neighbours(self):
        return self.tok_of(self.at(1)), self.tok_of(self.at(-1))

    def barrier(self, peers=1):
        sem = pltpu.get_barrier_semaphore()
        me = lax.axis_index("wid")
        for k in range(1, peers):
            other = lax.rem(me + k, peers)
            pl.semaphore_signal(
                sem, inc=1, device_id={"wid": other}, device_id_type=MESH
            )
        for other in self.neighbours():
            pl.semaphore_signal(
                sem, inc=1, device_id={"tok": other}, device_id_type=MESH
            )
        pl.semaphore_wait(sem, 1 + peers)


def wid_sum(m, part, got, mine, out, sems):
    me = lax.axis_index("wid")
    share = part.shape[0] // m

    def lines(index):
        return pl.ds(pl.multiple_of(index * share, 16), share)

    def copy(phase, k):
        other = lax.rem(me + k, m)
        return pltpu.make_async_remote_copy(
            src_ref=mine if phase else part.at[lines(other)],
            dst_ref=out.at[lines(me)] if phase else got.at[k - 1],
            send_sem=sems.at[phase, 0, k - 1],
            recv_sem=sems.at[phase, 1, k - 1],
            device_id={"wid": other},
            device_id_type=MESH,
        )

    for k in range(1, m):
        copy(0, k).start()
    total = part[lines(me), :]
    for k in range(1, m):
        copy(0, k).wait_recv()
        total = total + got[k - 1]
    mine[...] = total.astype(mine.dtype)
    for k in range(1, m):
        copy(1, k).start()
    out[lines(me), :] = total.astype(out.dtype)
    for k in range(1, m):
        copy(0, k).wait_send()
        copy(1, k).wait()


def ring_scatter(ring, term, store, send, recv, send_sems, recv_sems):
    n = ring.n
    dest = ring.neighbours()

    def copy(way, step, piece):
        return pltpu.make_async_remote_copy(
            src_ref=send.at[way, step, piece],
            dst_ref=recv.at[way, step, piece],
            send_sem=send_sems.at[way, step, piece],
            recv_sem=recv_sems.at[way, step, piece],
            device_id={"tok": dest[way]},
            device_id_type=MESH,
        )

    def block(way, step):
        return ring.at(-1 - step) if way == 0 else ring.at(1 + step)

    for piece in range(PIECES):
        for way in WAYS:
            send[way, 0, piece] = term(way, piece, block(way, 0)).astype(BF16)
            copy(way, 0, piece).start()

    def step(s, carry):
        for piece in range(PIECES):
            for way in WAYS:
                own = term(way, piece, block(way, s))
                copy(way, s - 1, piece).wait_recv()
                total = own + recv[way, s - 1, piece].astype(F32)
                send[way, s, piece] = total.astype(BF16)
                copy(way, s, piece).start()
        return carry

    lax.fori_loop(1, n - 1, step, 0)
    for piece in range(PIECES):
        for way in WAYS:
            own = term(way, piece, ring.pos)
            copy(way, n - 2, piece).wait_recv()
            store(way, piece, own + recv[way, n - 2, piece].astype(F32))

    def drain(s, carry):
        for piece in range(PIECES):
            for way in WAYS:
                copy(way, s, piece).wait_send()
        return carry

    lax.fori_loop(0, n - 1, drain, 0)


def sketch_kernel(
    n, m, acts, grads, test, out, part, got, mine, probe_t, wid_sems,
    send, recv, send_sems, recv_sems,
):
    ring = Ring(n)
    width = out.shape[1]
    rows = out.shape[0] // (2 * PIECES)

    def term(way, piece, pos):
        first = (way * PIECES + piece) * rows
        columns = pl.ds(pl.multiple_of(pos * width, 128), width)
        return jnp.dot(
            probe_t[first : first + rows, :], acts[:, columns], preferred_element_type=F32
        )

    def store(way, piece, total):
        first = (way * PIECES + piece) * rows
        out[first : first + rows, :] = total.astype(BF16)

    ring.barrier(m)
    part[...] = jnp.dot(grads[...], test[...], preferred_element_type=F32).T
    wid_sum(m, part, got, mine, probe_t, wid_sems)
    ring_scatter(ring, term, store, send, recv, send_sems, recv_sems)


def gather_kernel(
    n, m, acts, own, out_mixed, out_gram, part, got, mine, full, wid_sems,
    held, send_sems, recv_sems,
):
    tokens = acts.shape[0]
    mixed, gram = part.at[0:tokens], part.at[tokens : part.shape[0]]
    ring = Ring(n)
    width = own.shape[1]
    rows = own.shape[0] // (2 * PIECES)
    half = own.shape[0] // 2
    dest = ring.neighbours()

    def copy(way, step, piece, first=False):
        pos = ring.at(-step) if way == 0 else ring.at(step)
        lines = pl.ds((way * PIECES + piece) * rows, rows)
        return pltpu.make_async_remote_copy(
            src_ref=own.at[lines] if first else held.at[pos, lines],
            dst_ref=held.at[pos, lines],
            send_sem=send_sems.at[way, step, piece],
            recv_sem=recv_sems.at[way, step, piece],
            device_id={"tok": dest[way]},
            device_id_type=MESH,
        )

    def add(way, pos, ref):
        columns = pl.ds(pl.multiple_of(pos * width, 128), width)
        lanes = slice(way * half, (way + 1) * half)
        mixed[:, lanes] += nt(acts[:, columns], ref[lanes, :])

    def add_gram(pos):
        block = held.at[pos]
        gram[...] += nt(block[...], block[...])

    ring.barrier(m)
    for piece in range(PIECES):
        for way in WAYS:
            copy(way, 0, piece, True).start()
    mixed[...] = jnp.zeros_like(mixed)
    gram[...] = nt(own[...], own[...])
    for way in WAYS:
        add(way, ring.pos, own)

    def step(s, carry):
        for piece in range(PIECES):
            for way in WAYS:
                copy(way, s - 1, piece).wait_recv()
                copy(way, s, piece).start()
        for way in WAYS:
            pos = ring.at(-s) if way == 0 else ring.at(s)
            add(way, pos, held.at[pos])
        pl.when(2 * s >= n)(lambda: add_gram(ring.at(s)))
        pl.when(2 * s > n)(lambda: add_gram(ring.at(-s)))
        return carry

    lax.fori_loop(1, n - 1, step, 0)
    for piece in range(PIECES):
        for way in WAYS:
            copy(way, n - 2, piece).wait_recv()
    for way in WAYS:
        pos = ring.at(1 - n) if way == 0 else ring.at(n - 1)
        add(way, pos, held.at[pos])

    add_gram(ring.at(n - 1))
    add_gram(ring.at(1 - n))
    wid_sum(m, part, got, mine, full, wid_sems)
    out_mixed[...] = full[0:tokens, :]
    out_gram[...] = full[tokens : part.shape[0], :]

    def drain(s, carry):
        for piece in range(PIECES):
            for way in WAYS:
                copy(way, s, piece, False).wait_send()
        return carry

    lax.fori_loop(0, n - 1, drain, 0)


def invert(lower, inverse):
    i = lax.broadcasted_iota(jnp.int32, lower.shape, 0)
    j = lax.broadcasted_iota(jnp.int32, lower.shape, 1)
    inverse[...] = jnp.where(i == j, 1.0 / jnp.where(i == j, lower[...], 1.0), 0.0)

    def level(k, carry):
        i_block, j_block = lax.shift_right_logical(i, k), lax.shift_right_logical(j, k)
        same = lax.shift_right_logical(i, k + 1) == lax.shift_right_logical(j, k + 1)
        below = jnp.where(jnp.logical_and(same, i_block > j_block), lower[...], 0.0)
        high = lax.Precision.HIGHEST
        right = jnp.dot(below, inverse[...], precision=high, preferred_element_type=F32)
        inverse[...] -= jnp.dot(
            inverse[...], right, precision=high, preferred_element_type=F32
        )
        return carry

    lax.fori_loop(0, (lower.shape[0] - 1).bit_length(), level, 0)


def factor(gram, rest, upper):
    size = gram.shape[0]
    block = math.gcd(size, 32)
    lane = lax.broadcasted_iota(jnp.int32, (block, size), 1)
    line = lax.broadcasted_iota(jnp.int32, (block, size), 0)
    one_line = lax.broadcasted_iota(jnp.int32, (block, 1), 0)
    rest[...] = gram[...]

    def step(k, carry):
        first = pl.multiple_of(k * block, block)
        rows = rest[pl.ds(first, block), :]
        for j in range(block):
            picked = jnp.where(lane == first + j, rows, 0.0)
            column = jnp.sum(picked, axis=1, keepdims=True)
            ratio = jnp.where(one_line > j, column / column[j : j + 1, :], 0.0)
            rows = rows - ratio * rows[j : j + 1, :]
        diagonal = jnp.sum(
            jnp.where(lane == first + line, rows, 0.0), axis=1, keepdims=True
        )
        rows = jnp.where(lane >= first + line, rows / jnp.sqrt(diagonal), 0.0)
        upper[pl.ds(first, block), :] = rows
        rest[...] -= lax.dot_general(
            rows, rows, (((0,), (0,)), ((), ())),
            precision=lax.Precision.HIGHEST, preferred_element_type=F32,
        )
        return carry

    lax.fori_loop(0, size // block, step, 0)


def coeffs_kernel(
    n, scale, mixed, gram, grads, out, rest, lower, inverse, terms,
    send, recv, send_sems, recv_sems,
):
    ring = Ring(n)
    rows, width = out.shape
    part = width // (2 * PIECES)

    def term(way, piece, pos):
        first = (way * PIECES + piece) * part
        return terms[ring.tok_of(pos), :, first : first + part]

    def store(way, piece, total):
        first = (way * PIECES + piece) * part
        out[:, first : first + part] = total

    ring.barrier()
    factor(gram, rest, inverse)
    lower[...] = inverse[...].T
    invert(lower, inverse)
    proj_t = nt(inverse[...], mixed[...], lax.Precision.HIGHEST).astype(BF16)
    for first in range(0, width, 512 if width % 512 == 0 else width):
        last = min(width, first + 512) if width % 512 == 0 else width
        piece = jnp.dot(proj_t, grads[:, first:last], preferred_element_type=F32)
        terms[:, :, first:last] = (piece * scale).reshape(n, rows, last - first)
    ring_scatter(ring, term, store, send, recv, send_sems, recv_sems)


def call(kernel, outs, scratch, number, *args):
    vmem = pl.BlockSpec(memory_space=pltpu.VMEM)
    return pl.pallas_call(
        kernel,
        out_shape=outs,
        in_specs=[vmem] * len(args),
        out_specs=jax.tree.map(lambda _: vmem, outs),
        scratch_shapes=scratch,
        compiler_params=pltpu.CompilerParams(
            collective_id=number, has_side_effects=True, vmem_limit_bytes=VMEM_LIMIT
        ),
    )(*args)


def sems(n):
    return [pltpu.SemaphoreType.DMA((2, n - 1, PIECES)) for _ in range(2)]


def slots(n, rows, width):
    return [pltpu.VMEM((2, n - 1, PIECES, rows, width), BF16) for _ in range(2)]


def factor_inverse(gram):
    lower = jnp.linalg.cholesky(gram)
    eye_matrix = jnp.eye(gram.shape[0], dtype=F32)
    return lax.linalg.triangular_solve(lower, eye_matrix, left_side=True, lower=True)


def wid_scratch(m, rows, width, dtype):
    return [
        pltpu.VMEM((rows, width), F32),
        pltpu.VMEM((m - 1, rows // m, width), F32),
        pltpu.VMEM((rows // m, width), dtype),
        pltpu.VMEM((rows, width), dtype),
        pltpu.SemaphoreType.DMA((2, 2, m - 1)),
    ]


def ring_shards(n, m, acts, out_grads, test_matrix):
    tokens, hidden = acts.shape
    rank, model = test_matrix.shape[1], out_grads.shape[1]
    width = hidden // n
    struct = jax.ShapeDtypeStruct
    rows_t = call(
        functools.partial(sketch_kernel, n, m),
        struct((rank, width), BF16),
        wid_scratch(m, rank, tokens, BF16)
        + slots(n, rank // (2 * PIECES), width) + sems(n),
        0, acts, out_grads, test_matrix,
    )
    mixed, gram = call(
        functools.partial(gather_kernel, n, m),
        [struct((tokens, rank), F32), struct((rank, rank), F32)],
        wid_scratch(m, tokens + rank, rank, F32)
        + [pltpu.VMEM((n, rank, width), BF16)] + sems(n),
        1, acts, rows_t,
    )
    scale = 1.0 / math.sqrt(tokens * n)
    rows = rank // n
    return call(
        functools.partial(coeffs_kernel, n, scale),
        struct((rows, model), F32),
        [pltpu.VMEM((rank, rank), F32) for _ in range(3)]
        + [pltpu.VMEM((n, rows, model), F32)]
        + slots(n, rows, model // (2 * PIECES)) + sems(n),
        2, mixed, gram, out_grads,
    )


def plain_shards(acts, out_grads, test_matrix):
    partial_probe = jnp.dot(out_grads, test_matrix, preferred_element_type=F32)
    probe = lax.psum(partial_probe, "wid").astype(BF16)
    local_sketch = lax.dot_general(
        acts, probe, (((0,), (0,)), ((), ())), preferred_element_type=F32
    )
    sketch = lax.psum(local_sketch.astype(BF16), "tok")
    gram = lax.psum(
        lax.dot_general(sketch, sketch, (((0,), (0,)), ((), ())), preferred_element_type=F32),
        "wid",
    )
    inverse = factor_inverse(gram)
    mixed = lax.psum(jnp.dot(acts, sketch, preferred_element_type=F32), "wid")
    proj = jnp.dot(mixed, inverse.T, precision=lax.Precision.HIGHEST).astype(BF16)
    scale = 1.0 / math.sqrt(acts.shape[0] * lax.axis_size("tok"))
    term = lax.dot_general(
        proj, out_grads, (((0,), (0,)), ((), ())), preferred_element_type=F32
    )
    return lax.psum_scatter(term * scale, "tok", scatter_dimension=0, tiled=True)


def solution(mesh):
    n, m = mesh.shape["tok"], mesh.shape["wid"]

    def shards(acts, out_grads, test_matrix):
        width, left = divmod(acts.shape[1], n)
        even = acts.shape[0] % (16 * m) == 0 and test_matrix.shape[1] % (16 * m) == 0
        if n % 4 == 0 and n > 4 and m > 1 and even and left == 0 and width % 128 == 0:
            return ring_shards(n, m, acts, out_grads, test_matrix)
        return plain_shards(acts, out_grads, test_matrix)

    return jax.shard_map(
        shards,
        mesh=mesh,
        in_specs=(P("tok", "wid"), P("tok", "wid"), P("wid", None)),
        out_specs=P("tok", "wid"),
        check_vma=False,
    )
```

```python
import functools
import math

import jax
import jax.numpy as jnp
from jax import lax
from jax.experimental import pallas as pl
from jax.experimental.pallas import tpu as pltpu
from jax.sharding import PartitionSpec as P

MESH = pl.DeviceIdType.MESH
F32 = jnp.float32
BF16 = jnp.bfloat16
VMEM_LIMIT = 60 * 1024 * 1024
WAYS = (0, 1)
PIECES = 4


def nt(a, b, precision=None):
    return lax.dot_general(
        a, b, (((1,), (1,)), ((), ())), preferred_element_type=F32, precision=precision
    )


class Ring:
    def __init__(self, n):
        self.n, self.rows, self.cols = n, 4, n // 4
        self.body = self.rows * (self.cols - 1)
        self.tok = lax.axis_index("tok")
        self.pos = self.pos_of(self.tok)

    def pos_of(self, tok):
        r, c = lax.div(tok, self.cols), lax.rem(tok, self.cols)
        odd = lax.rem(r, 2)
        inner = lax.div(c + self.cols - 1, self.cols)
        along = r * (self.cols - 1) + (1 - odd) * (c - 1) + odd * (self.cols - 1 - c)
        back = self.body + self.rows - 1 - r
        return inner * along + (1 - inner) * back

    def tok_of(self, pos):
        last = lax.div(pos, self.body)
        r, k = lax.div(pos, self.cols - 1), lax.rem(pos, self.cols - 1)
        odd = lax.rem(r, 2)
        along = r * self.cols + (1 - odd) * (k + 1) + odd * (self.cols - 1 - k)
        back = (self.rows - 1 - (pos - self.body)) * self.cols
        return (1 - last) * along + last * back

    def at(self, offset):
        return lax.rem(self.pos + offset + 2 * self.n, self.n)

    def neighbours(self):
        return self.tok_of(self.at(1)), self.tok_of(self.at(-1))

    def barrier(self, peers=1):
        sem = pltpu.get_barrier_semaphore()
        me = lax.axis_index("wid")
        for k in range(1, peers):
            other = lax.rem(me + k, peers)
            pl.semaphore_signal(
                sem, inc=1, device_id={"wid": other}, device_id_type=MESH
            )
        for other in self.neighbours():
            pl.semaphore_signal(
                sem, inc=1, device_id={"tok": other}, device_id_type=MESH
            )
        pl.semaphore_wait(sem, 1 + peers)


def wid_sum(m, part, got, mine, out, sems):
    me = lax.axis_index("wid")
    share = part.shape[0] // m

    def lines(index):
        return pl.ds(pl.multiple_of(index * share, 16), share)

    def copy(phase, k):
        other = lax.rem(me + k, m)
        return pltpu.make_async_remote_copy(
            src_ref=mine if phase else part.at[lines(other)],
            dst_ref=out.at[lines(me)] if phase else got.at[k - 1],
            send_sem=sems.at[phase, 0, k - 1],
            recv_sem=sems.at[phase, 1, k - 1],
            device_id={"wid": other},
            device_id_type=MESH,
        )

    for k in range(1, m):
        copy(0, k).start()
    total = part[lines(me), :]
    for k in range(1, m):
        copy(0, k).wait_recv()
        total = total + got[k - 1]
    mine[...] = total.astype(mine.dtype)
    for k in range(1, m):
        copy(1, k).start()
    out[lines(me), :] = total.astype(out.dtype)
    for k in range(1, m):
        copy(0, k).wait_send()
        copy(1, k).wait()


def ring_scatter(ring, term, store, send, recv, send_sems, recv_sems):
    n = ring.n
    dest = ring.neighbours()

    def copy(way, step, piece):
        return pltpu.make_async_remote_copy(
            src_ref=send.at[way, step, piece],
            dst_ref=recv.at[way, step, piece],
            send_sem=send_sems.at[way, step, piece],
            recv_sem=recv_sems.at[way, step, piece],
            device_id={"tok": dest[way]},
            device_id_type=MESH,
        )

    def block(way, step):
        return ring.at(-1 - step) if way == 0 else ring.at(1 + step)

    for piece in range(PIECES):
        for way in WAYS:
            send[way, 0, piece] = term(way, piece, block(way, 0)).astype(BF16)
            copy(way, 0, piece).start()

    def step(s, carry):
        for piece in range(PIECES):
            for way in WAYS:
                own = term(way, piece, block(way, s))
                copy(way, s - 1, piece).wait_recv()
                total = own + recv[way, s - 1, piece].astype(F32)
                send[way, s, piece] = total.astype(BF16)
                copy(way, s, piece).start()
        return carry

    lax.fori_loop(1, n - 1, step, 0)
    for piece in range(PIECES):
        for way in WAYS:
            own = term(way, piece, ring.pos)
            copy(way, n - 2, piece).wait_recv()
            store(way, piece, own + recv[way, n - 2, piece].astype(F32))

    def drain(s, carry):
        for piece in range(PIECES):
            for way in WAYS:
                copy(way, s, piece).wait_send()
        return carry

    lax.fori_loop(0, n - 1, drain, 0)


def sketch_kernel(
    n, m, acts, grads, test, out, part, got, mine, probe_t, wid_sems,
    send, recv, send_sems, recv_sems,
):
    ring = Ring(n)
    width = out.shape[1]
    rows = out.shape[0] // (2 * PIECES)

    def term(way, piece, pos):
        first = (way * PIECES + piece) * rows
        columns = pl.ds(pl.multiple_of(pos * width, 128), width)
        return jnp.dot(
            probe_t[first : first + rows, :], acts[:, columns], preferred_element_type=F32
        )

    def store(way, piece, total):
        first = (way * PIECES + piece) * rows
        out[first : first + rows, :] = total.astype(BF16)

    ring.barrier(m)
    part[...] = jnp.dot(grads[...], test[...], preferred_element_type=F32).T
    wid_sum(m, part, got, mine, probe_t, wid_sems)
    ring_scatter(ring, term, store, send, recv, send_sems, recv_sems)


def gather_kernel(
    n, m, acts, own, out_mixed, out_gram, part, got, mine, full, wid_sems,
    held, send_sems, recv_sems,
):
    tokens = acts.shape[0]
    mixed, gram = part.at[0:tokens], part.at[tokens : part.shape[0]]
    ring = Ring(n)
    width = own.shape[1]
    rows = own.shape[0] // (2 * PIECES)
    half = own.shape[0] // 2
    dest = ring.neighbours()

    def copy(way, step, piece, first=False):
        pos = ring.at(-step) if way == 0 else ring.at(step)
        lines = pl.ds((way * PIECES + piece) * rows, rows)
        return pltpu.make_async_remote_copy(
            src_ref=own.at[lines] if first else held.at[pos, lines],
            dst_ref=held.at[pos, lines],
            send_sem=send_sems.at[way, step, piece],
            recv_sem=recv_sems.at[way, step, piece],
            device_id={"tok": dest[way]},
            device_id_type=MESH,
        )

    def add(way, pos, ref):
        columns = pl.ds(pl.multiple_of(pos * width, 128), width)
        lanes = slice(way * half, (way + 1) * half)
        mixed[:, lanes] += nt(acts[:, columns], ref[lanes, :])

    def add_gram(pos):
        block = held.at[pos]
        gram[...] += nt(block[...], block[...])

    ring.barrier(m)
    for piece in range(PIECES):
        for way in WAYS:
            copy(way, 0, piece, True).start()
    mixed[...] = jnp.zeros_like(mixed)
    gram[...] = nt(own[...], own[...])
    for way in WAYS:
        add(way, ring.pos, own)

    def step(s, carry):
        for piece in range(PIECES):
            for way in WAYS:
                copy(way, s - 1, piece).wait_recv()
                copy(way, s, piece).start()
        for way in WAYS:
            pos = ring.at(-s) if way == 0 else ring.at(s)
            add(way, pos, held.at[pos])
        pl.when(2 * s >= n)(lambda: add_gram(ring.at(s)))
        pl.when(2 * s > n)(lambda: add_gram(ring.at(-s)))
        return carry

    lax.fori_loop(1, n - 1, step, 0)
    for piece in range(PIECES):
        for way in WAYS:
            copy(way, n - 2, piece).wait_recv()
    for way in WAYS:
        pos = ring.at(1 - n) if way == 0 else ring.at(n - 1)
        add(way, pos, held.at[pos])

    add_gram(ring.at(n - 1))
    add_gram(ring.at(1 - n))
    wid_sum(m, part, got, mine, full, wid_sems)
    out_mixed[...] = full[0:tokens, :]
    out_gram[...] = full[tokens : part.shape[0], :]

    def drain(s, carry):
        for piece in range(PIECES):
            for way in WAYS:
                copy(way, s, piece, False).wait_send()
        return carry

    lax.fori_loop(0, n - 1, drain, 0)


def invert(lower, inverse):
    i = lax.broadcasted_iota(jnp.int32, lower.shape, 0)
    j = lax.broadcasted_iota(jnp.int32, lower.shape, 1)
    inverse[...] = jnp.where(i == j, 1.0 / jnp.where(i == j, lower[...], 1.0), 0.0)

    def level(k, carry):
        i_block, j_block = lax.shift_right_logical(i, k), lax.shift_right_logical(j, k)
        same = lax.shift_right_logical(i, k + 1) == lax.shift_right_logical(j, k + 1)
        below = jnp.where(jnp.logical_and(same, i_block > j_block), lower[...], 0.0)
        high = lax.Precision.HIGHEST
        right = jnp.dot(below, inverse[...], precision=high, preferred_element_type=F32)
        inverse[...] -= jnp.dot(
            inverse[...], right, precision=high, preferred_element_type=F32
        )
        return carry

    lax.fori_loop(0, (lower.shape[0] - 1).bit_length(), level, 0)


def factor(gram, rest, upper):
    size = gram.shape[0]
    block = math.gcd(size, 32)
    lane = lax.broadcasted_iota(jnp.int32, (block, size), 1)
    line = lax.broadcasted_iota(jnp.int32, (block, size), 0)
    one_line = lax.broadcasted_iota(jnp.int32, (block, 1), 0)
    rest[...] = gram[...]

    def step(k, carry):
        first = pl.multiple_of(k * block, block)
        rows = rest[pl.ds(first, block), :]
        for j in range(block):
            picked = jnp.where(lane == first + j, rows, 0.0)
            column = jnp.sum(picked, axis=1, keepdims=True)
            ratio = jnp.where(one_line > j, column / column[j : j + 1, :], 0.0)
            rows = rows - ratio * rows[j : j + 1, :]
        diagonal = jnp.sum(
            jnp.where(lane == first + line, rows, 0.0), axis=1, keepdims=True
        )
        rows = jnp.where(lane >= first + line, rows / jnp.sqrt(diagonal), 0.0)
        upper[pl.ds(first, block), :] = rows
        rest[...] -= lax.dot_general(
            rows, rows, (((0,), (0,)), ((), ())),
            precision=lax.Precision.HIGHEST, preferred_element_type=F32,
        )
        return carry

    lax.fori_loop(0, size // block, step, 0)


def coeffs_kernel(
    n, scale, mixed, gram, grads, out, rest, lower, inverse, terms,
    send, recv, send_sems, recv_sems,
):
    ring = Ring(n)
    rows, width = out.shape
    part = width // (2 * PIECES)

    def term(way, piece, pos):
        first = (way * PIECES + piece) * part
        return terms[ring.tok_of(pos), :, first : first + part]

    def store(way, piece, total):
        first = (way * PIECES + piece) * part
        out[:, first : first + part] = total

    ring.barrier()
    factor(gram, rest, inverse)
    lower[...] = inverse[...].T
    invert(lower, inverse)
    proj_t = nt(inverse[...], mixed[...], lax.Precision.HIGHEST).astype(BF16)
    for first in range(0, width, 512 if width % 512 == 0 else width):
        last = min(width, first + 512) if width % 512 == 0 else width
        piece = jnp.dot(proj_t, grads[:, first:last], preferred_element_type=F32)
        terms[:, :, first:last] = (piece * scale).reshape(n, rows, last - first)
    ring_scatter(ring, term, store, send, recv, send_sems, recv_sems)


def call(kernel, outs, scratch, number, *args):
    vmem = pl.BlockSpec(memory_space=pltpu.VMEM)
    return pl.pallas_call(
        kernel,
        out_shape=outs,
        in_specs=[vmem] * len(args),
        out_specs=jax.tree.map(lambda _: vmem, outs),
        scratch_shapes=scratch,
        compiler_params=pltpu.CompilerParams(
            collective_id=number, has_side_effects=True, vmem_limit_bytes=VMEM_LIMIT
        ),
    )(*args)


def sems(n):
    return [pltpu.SemaphoreType.DMA((2, n - 1, PIECES)) for _ in range(2)]


def slots(n, rows, width):
    return [pltpu.VMEM((2, n - 1, PIECES, rows, width), BF16) for _ in range(2)]


def factor_inverse(gram):
    lower = jnp.linalg.cholesky(gram)
    eye_matrix = jnp.eye(gram.shape[0], dtype=F32)
    return lax.linalg.triangular_solve(lower, eye_matrix, left_side=True, lower=True)


def wid_scratch(m, rows, width, dtype):
    return [
        pltpu.VMEM((rows, width), F32),
        pltpu.VMEM((m - 1, rows // m, width), F32),
        pltpu.VMEM((rows // m, width), dtype),
        pltpu.VMEM((rows, width), dtype),
        pltpu.SemaphoreType.DMA((2, 2, m - 1)),
    ]


def ring_shards(n, m, acts, out_grads, test_matrix):
    tokens, hidden = acts.shape
    rank, model = test_matrix.shape[1], out_grads.shape[1]
    width = hidden // n
    struct = jax.ShapeDtypeStruct
    rows_t = call(
        functools.partial(sketch_kernel, n, m),
        struct((rank, width), BF16),
        wid_scratch(m, rank, tokens, BF16)
        + slots(n, rank // (2 * PIECES), width) + sems(n),
        0, acts, out_grads, test_matrix,
    )
    mixed, gram = call(
        functools.partial(gather_kernel, n, m),
        [struct((tokens, rank), F32), struct((rank, rank), F32)],
        wid_scratch(m, tokens + rank, rank, F32)
        + [pltpu.VMEM((n, rank, width), BF16)] + sems(n),
        1, acts, rows_t,
    )
    scale = 1.0 / math.sqrt(tokens * n)
    rows = rank // n
    return call(
        functools.partial(coeffs_kernel, n, scale),
        struct((rows, model), F32),
        [pltpu.VMEM((rank, rank), F32) for _ in range(3)]
        + [pltpu.VMEM((n, rows, model), F32)]
        + slots(n, rows, model // (2 * PIECES)) + sems(n),
        2, mixed, gram, out_grads,
    )


def plain_shards(acts, out_grads, test_matrix):
    partial_probe = jnp.dot(out_grads, test_matrix, preferred_element_type=F32)
    probe = lax.psum(partial_probe, "wid").astype(BF16)
    local_sketch = lax.dot_general(
        acts, probe, (((0,), (0,)), ((), ())), preferred_element_type=F32
    )
    sketch = lax.psum(local_sketch.astype(BF16), "tok")
    gram = lax.psum(
        lax.dot_general(sketch, sketch, (((0,), (0,)), ((), ())), preferred_element_type=F32),
        "wid",
    )
    inverse = factor_inverse(gram)
    mixed = lax.psum(jnp.dot(acts, sketch, preferred_element_type=F32), "wid")
    proj = jnp.dot(mixed, inverse.T, precision=lax.Precision.HIGHEST).astype(BF16)
    scale = 1.0 / math.sqrt(acts.shape[0] * lax.axis_size("tok"))
    term = lax.dot_general(
        proj, out_grads, (((0,), (0,)), ((), ())), preferred_element_type=F32
    )
    return lax.psum_scatter(term * scale, "tok", scatter_dimension=0, tiled=True)


def solution(mesh):
    n, m = mesh.shape["tok"], mesh.shape["wid"]

    def shards(acts, out_grads, test_matrix):
        width, left = divmod(acts.shape[1], n)
        even = acts.shape[0] % (16 * m) == 0 and test_matrix.shape[1] % (16 * m) == 0
        if n % 4 == 0 and n > 4 and m > 1 and even and left == 0 and width % 128 == 0:
            return ring_shards(n, m, acts, out_grads, test_matrix)
        return plain_shards(acts, out_grads, test_matrix)

    return jax.shard_map(
        shards,
        mesh=mesh,
        in_specs=(P("tok", "wid"), P("tok", "wid"), P("wid", None)),
        out_specs=P("tok", "wid"),
        check_vma=False,
    )
```
